32 devices in a mesh: grp: 2 (over core), brick: 16 (over z, y, x).
Axes of the slice: x: 2, y: 2, z: 4, core: 2. Of those that a mesh axis runs over, the one named last changes fastest.
Arguments:
- density: float32 [64, 64, 256], P('brick', None, 'grp'), may hold values from 0.5 to 2
- energy_field: float32 [64, 64, 256], P('brick', None, 'grp'), may hold values from -6 to 6
- lepton_field: float32 [64, 64, 256], P('brick', None, 'grp'), may hold values from 0.1 to 0.6
- velocity: float32 [3, 64, 64, 256], P(None, 'brick', None, 'grp'), may hold values from -4 to 4
- abundance: float32 [2, 16, 1024, 128], P('grp', 'brick'), may hold values from -1.2 to 1.2
- tracer_mass: float32 [2, 16, 1024], P('grp', 'brick'), may hold values from 0.2 to 1
- tracer_cell: int32 [2, 16, 1024], P('grp', 'brick'), may hold values from 0 to 32767
- tracer_count: int32 [2, 16], P('grp', 'brick'), may hold values from 1 to 1024, as said below
- weak_rates: float32 [128, 128], replicated, may hold values from -0.5 to 0.5
- capture_rates: float32 [128, 128], replicated, may hold values from -0.5 to 0.5
- binding: float32 [128], replicated, may hold values from -6 to 6
- charge_ratio: float32 [128], replicated, may hold values from 0 to 1
Outputs:
- density_out: float32 [64, 64, 256], P('brick', None, 'grp')
- energy_out: float32 [64, 64, 256], P('brick', None, 'grp')
- lepton_out: float32 [64, 64, 256], P('brick', None, 'grp')
- abundance_out: float32 [2, 16, 1024, 128], P('grp', 'brick')
The draws below stay inside these ranges and needn't reach their ends.
Inputs may be any that keep to these rules, and one draw needn't show every extreme that they name: `tracer_count`: for each index of grp the counts sum to 8192; exactly one brick of each half holds 1024, the most; every other brick holds at most 512, and some brick of each half holds exactly 512.
All inputs are finite; a program needn't handle non-finite values.
Results may differ from the reference program's by a relative error of at most 0.00029.
Values sent between devices are 32-bit elements; how exact they have to be, the bound alone decides.
A program may use at most 64 MiB of HBM per device.

```python
import math
import jax
import jax.numpy as jnp
from jax import lax

S = 128
CX = 4
CY = 64
CZ = 128
TR_DEV = 512
NEWTON = 2
SWEEPS = 8
TCAP = 1024
NX = 64
NZ = 256
N_GRP = 2
N_BRICK = 16


def draw_tracer_count(key, part):
    first_key, second_key, third_key = jax.random.split(key, 3)
    busiest = jax.random.randint(first_key, (N_GRP,), 0, N_BRICK)
    offset = jax.random.randint(third_key, (N_GRP,), 1, N_BRICK)
    filled = (busiest + offset) % N_BRICK
    weights = jax.random.randint(second_key, (N_GRP, N_BRICK), 1, 4)
    brick_ids = jnp.arange(N_BRICK, dtype=jnp.int32)[None, :]
    is_busiest = brick_ids == busiest[:, None]
    is_filled = brick_ids == filled[:, None]
    others = jnp.logical_not(jnp.logical_or(is_busiest, is_filled)).astype(jnp.int32)
    weights = weights * others
    shares = weights * TR_DEV // jnp.sum(weights, axis=1, keepdims=True)
    leftover = TR_DEV - jnp.sum(shares, axis=1, keepdims=True)
    rank_order = jnp.cumsum(others, axis=1) - 1
    shares = shares + others * (rank_order < leftover).astype(jnp.int32)
    return jnp.where(is_busiest, TCAP, TR_DEV - shares).astype(jnp.int32)


def with_ends(array, stream_key, smallest, top_value):
    shape = array.shape
    place = [jax.random.randint(jax.random.fold_in(stream_key, axis), (), 0, shape[axis]) for axis in range(len(shape))]
    array = array.at[tuple(place)].set(smallest)
    longest = shape.index(max(shape))
    place[longest] = (place[longest] + 1) % shape[longest]
    return array.at[tuple(place)].set(top_value)


def block_scale(own_key, shape, pieces, smallest, high):
    loudness = 1.0
    for axis_at, shards_of in pieces:
        heights = jax.random.uniform(jax.random.fold_in(jax.random.fold_in(own_key, 6), axis_at), (shards_of,), jnp.float32, smallest / len(pieces), high / len(pieces))
        loudness = loudness * jnp.repeat(jnp.exp(heights), shape[axis_at] // shards_of).reshape((-1,) + (1,) * (len(shape) - 1 - axis_at))
    return loudness


def centred(stream_key, extent, deviation, bound, cuts=(), kind=jnp.bfloat16):
    values = deviation * jax.random.normal(stream_key, extent, jnp.float32)
    if cuts:
        values = values * block_scale(stream_key, extent, cuts, -0.22, 0.18)
    return jnp.clip(values, -bound, bound).astype(kind)


def setup_inputs(seed: int = 0) -> dict:
    keys = jax.random.split(jax.random.key(seed), 13)
    return {
        "density": jnp.clip(jnp.exp(math.log(2.0) - 1.3862944 * jax.random.uniform(keys[0], (NX, CY, NZ), jnp.float32) ** block_scale(keys[0], (NX, CY, NZ), ((0, 16), (2, 2)), -0.2, 0.2)), 0.5, 2.0),
        "energy_field": centred(keys[1], (NX, CY, NZ), 1.0, 6.0, ((0, 16), (2, 2)), jnp.float32),
        "lepton_field": jnp.clip(0.1 + 0.5 * jax.random.uniform(keys[2], (NX, CY, NZ), jnp.float32) ** block_scale(keys[2], (NX, CY, NZ), ((0, 16), (2, 2)), -0.2, 0.2), 0.1, 0.6),
        "velocity": centred(keys[3], (3, NX, CY, NZ), 1.0, 4.0, ((1, 16), (3, 2)), jnp.float32),
        "abundance": centred(keys[4], (N_GRP, N_BRICK, TCAP, S), 0.3, 1.2, ((0, 2), (1, 16)), jnp.float32),
        "tracer_mass": jnp.clip(jnp.exp(math.log(1.0) - 1.609438 * jax.random.uniform(keys[5], (N_GRP, N_BRICK, TCAP), jnp.float32) ** block_scale(keys[5], (N_GRP, N_BRICK, TCAP), ((0, 2), (1, 16)), -0.2, 0.2)), 0.2, 1.0),
        "tracer_cell": with_ends(jax.random.randint(keys[6], (N_GRP, N_BRICK, TCAP), 0, CX * CY * CZ), jax.random.fold_in(keys[6], 1), 0, (CX * CY * CZ) - 1).astype(jnp.int32),
        "tracer_count": draw_tracer_count(jax.random.fold_in(keys[12], 71), 0),
        "weak_rates": centred(keys[8], (S, S), S ** -0.5, 0.5, (), jnp.float32),
        "capture_rates": centred(keys[9], (S, S), S ** -0.5, 0.5, (), jnp.float32),
        "binding": centred(keys[10], (S,), 1.0, 6.0, (), jnp.float32),
        "charge_ratio": jnp.clip(jax.random.uniform(keys[11], (S,), jnp.float32, 0.0, 1.0), 0.0, 1.0),
    }


courant = 0.8
highest = lax.Precision.HIGHEST


def rolled_difference(values, axis_number):
    return (8.0 * (jnp.roll(values, -1, axis_number) - jnp.roll(values, 1, axis_number)) - (jnp.roll(values, -2, axis_number) - jnp.roll(values, 2, axis_number))) / 12.0


def full_tendency(fields, speeds):
    along_x = rolled_difference(speeds[0][None] * fields, 1)
    along_y = rolled_difference(speeds[1][None] * fields, 2)
    along_z = rolled_difference(speeds[2][None] * fields, 3)
    return -((along_x + along_y) + along_z)


def thermo_rates(density, energy_field, lepton_field, cells):
    thermo = jnp.stack([density, energy_field, lepton_field]).reshape(3, -1)
    picked = jnp.take(thermo, cells, axis=1)
    weak_scale = 0.62 + 0.04 * picked[0] + 0.05 * (picked[2] / picked[0])
    capture_scale = 0.3 * jax.nn.sigmoid(picked[1] / picked[0])
    return weak_scale, capture_scale


def network_step(initial, rate_weak, rate_capture, matrices):
    species = initial.shape[1]
    iterate = initial
    for newton_turn in range(NEWTON):
        products = jnp.dot(iterate, matrices, precision=highest, preferred_element_type=jnp.float32)
        alpha_part = iterate[:, 0:1]
        capture = products[:, species:]
        target = -(iterate - initial - (rate_weak * products[:, :species] + rate_capture * alpha_part * capture))
        update = target
        for sweep_turn in range(SWEEPS):
            product = jnp.dot(update, matrices, precision=highest, preferred_element_type=jnp.float32)
            update = target + (rate_weak * product[:, :species] + rate_capture * alpha_part * product[:, species:] + rate_capture * update[:, 0:1] * capture)
        iterate = iterate + update
    return iterate


def reference(density, energy_field, lepton_field, velocity, abundance, tracer_mass, tracer_cell, tracer_count, weak_rates, capture_rates, binding, charge_ratio):
    state = jnp.stack([density, energy_field, lepton_field])
    midpoint = state + (0.5 * courant) * full_tendency(state, velocity)
    advanced = state + courant * full_tendency(midpoint, velocity)
    groups_z, groups_x, capacity = tracer_cell.shape
    plane = CY * CZ
    cell_x = tracer_cell // plane
    cell_y = (tracer_cell // CZ) % CY
    cell_z = tracer_cell % CZ
    grp_ids = jnp.arange(groups_z, dtype=jnp.int32)[:, None, None]
    brick_ids = jnp.arange(groups_x, dtype=jnp.int32)[None, :, None]
    global_cell = ((brick_ids * CX + cell_x) * CY + cell_y) * NZ + grp_ids * CZ + cell_z
    flat_ids = global_cell.reshape(-1).astype(jnp.int32)
    weak_scale, capture_scale = thermo_rates(density, energy_field, lepton_field, flat_ids)
    occupied = (jnp.arange(capacity, dtype=jnp.int32)[None, None, :] < tracer_count[:, :, None]).reshape(-1, capacity)
    rows = abundance.reshape(-1, capacity, S)
    rates = jnp.stack([weak_scale, capture_scale], axis=1).reshape(-1, capacity, 2)
    matrices = jnp.concatenate([weak_rates, capture_rates], axis=1)

    def solve_block(block_item):
        return network_step(block_item[0], block_item[1][:, 0:1], block_item[1][:, 1:2], matrices)

    solved = lax.map(solve_block, (rows, rates))
    finished = jnp.where(occupied[..., None], solved, 0.0)
    initial = jnp.where(occupied[..., None], rows, 0.0)
    change = (finished - initial).reshape(-1, S)
    table = jnp.stack([binding, charge_ratio], axis=1)
    gains = jnp.dot(change, table, precision=highest, preferred_element_type=jnp.float32) * tracer_mass.reshape(-1)[:, None]
    deposit = jnp.zeros((NX * CY * NZ, 2), jnp.float32).at[flat_ids].add(gains)
    energy_out = advanced[1] + deposit[:, 0].reshape(NX, CY, NZ)
    lepton_out = advanced[2] + deposit[:, 1].reshape(NX, CY, NZ)
    return advanced[0], energy_out, lepton_out, finished.reshape(abundance.shape)
```

```python
import functools

import jax
import jax.numpy as jnp
from jax import lax
from jax.experimental import pallas as pl
from jax.experimental.pallas import tpu as pltpu
from jax.sharding import PartitionSpec as P

NEWTON = 2
SWEEPS = 8
courant = 0.8
f32 = jnp.float32
bf16 = jnp.bfloat16
BLOCK = 256
EARLY = 2
MESH = pl.DeviceIdType.MESH


def split(values):
    high = values.astype(bf16)
    low = (values - high.astype(f32)).astype(bf16)
    return high, low


def dot(a, b, dims=((1,), (0,))):
    return lax.dot_general(a, b, (dims, ((), ())), preferred_element_type=f32)


def five_point(lower2, lower1, upper1, upper2):
    return 8.0 * (upper1 - lower1) - (upper2 - lower2)


def y_part(g):
    n = g.shape[0]
    return five_point(
        pltpu.roll(g, 2, 0), pltpu.roll(g, 1, 0), pltpu.roll(g, n - 1, 0), pltpu.roll(g, n - 2, 0)
    )


def z_part(h, other):
    n = h.shape[1]
    lane = lax.broadcasted_iota(jnp.int32, h.shape, 1)
    return five_point(
        pltpu.roll(jnp.where(lane >= n - 2, other, h), 2, 1),
        pltpu.roll(jnp.where(lane >= n - 1, other, h), 1, 1),
        pltpu.roll(jnp.where(lane < 1, other, h), n - 1, 1),
        pltpu.roll(jnp.where(lane < 2, other, h), n - 2, 1),
    )


def kernel(
    axis_sizes,
    count_hbm,
    rho_hbm,
    eps_hbm,
    lam_hbm,
    vel_hbm,
    rows_hbm,
    mass_hbm,
    cell_hbm,
    weak_hbm,
    capture_hbm,
    binding_hbm,
    charge_hbm,
    density_out,
    energy_out,
    lepton_out,
    abundance_out,
    count_ref,
    field,
    vel,
    mass_ref,
    cell_ref,
    rates,
    table,
    xs,
    zs,
    low_in,
    high_in,
    z_in,
    v_in,
    mid,
    weights,
    onehot,
    rate_weak,
    rate_capture,
    start_rows,
    alpha_capture,
    scaled_capture,
    target,
    update,
    deposit,
    load_sem,
    send_sem,
    recv_sem,
    z_send_sem,
    z_recv_sem,
    v_sem,
):
    n_grp, n_brick = axis_sizes
    g = lax.axis_index("grp")
    b = lax.axis_index("brick")
    last = n_brick - 1
    right = (g, lax.rem(b + 1, n_brick))
    left = (g, lax.rem(b + n_brick - 1, n_brick))
    partner = (lax.rem(g + 1, n_grp), b)
    outs = (density_out, energy_out, lepton_out)
    cx, cy, cz = density_out.shape
    capacity, species = abundance_out.shape
    assert cx == 4
    low_pair = pl.ds(0, 2)
    high_pair = pl.ds(cx - 2, 2)
    pairs = (low_pair, high_pair)

    barrier = pltpu.get_barrier_semaphore()

    def greet(device):
        pl.semaphore_signal(barrier, inc=1, device_id=device, device_id_type=MESH)

    greet(partner)

    @pl.when(b > 0)
    def _():
        greet(left)

    @pl.when(b < last)
    def _():
        greet(right)

    moves = [
        pltpu.make_async_copy(src, dst, load_sem.at[k])
        for k, (src, dst) in enumerate(
            (
                (vel_hbm.at[0], vel.at[0]),
                (rho_hbm, field.at[0]),
                (eps_hbm, field.at[1]),
                (lam_hbm, field.at[2]),
                (vel_hbm.at[2], vel.at[2]),
                (cell_hbm, cell_ref),
                (vel_hbm.at[1], vel.at[1]),
                (weak_hbm, rates.at[0]),
                (capture_hbm, rates.at[1]),
                (count_hbm, count_ref),
                (rows_hbm, start_rows),
                (mass_hbm, mass_ref),
                (binding_hbm, table.at[pl.ds(0, 1)]),
                (charge_hbm, table.at[pl.ds(1, 1)]),
            )
        )
    ]
    for move in moves:
        move.start()

    def x_copy(stage, f, side):
        src, dst, device = (
            (xs.at[stage, f, low_pair], high_in.at[stage, f], left),
            (xs.at[stage, f, high_pair], low_in.at[stage, f], right),
        )[side]
        return pltpu.make_async_remote_copy(
            src_ref=src,
            dst_ref=dst,
            send_sem=send_sem.at[stage, f, side],
            recv_sem=recv_sem.at[stage, f, side],
            device_id=device,
            device_id_type=MESH,
        )

    def z_copy(stage, f, side):
        return pltpu.make_async_remote_copy(
            src_ref=zs.at[stage, f, pairs[side]],
            dst_ref=z_in.at[stage, f, pairs[side]],
            send_sem=z_send_sem.at[stage, f, side],
            recv_sem=z_recv_sem.at[stage, f, side],
            device_id=partner,
            device_id_type=MESH,
        )

    def v_copy():
        return pltpu.make_async_remote_copy(
            src_ref=vel.at[0, high_pair],
            dst_ref=v_in,
            send_sem=v_sem.at[0],
            recv_sem=v_sem.at[1],
            device_id=right,
            device_id_type=MESH,
        )

    moves[0].wait()
    for f in range(3):
        moves[1 + f].wait()
        for p in range(cx):
            xs[0, f, p] = vel[0, p] * field[f, p]

    @pl.when(b == 0)
    def _():
        pl.semaphore_wait(barrier, 2)
        greet(left)

    @pl.when(b > 0)
    def _():
        pl.semaphore_wait(barrier, 3)

    @pl.when(b == last)
    def _():
        greet(right)

    for f in range(3):
        x_copy(0, f, 1).start()

        @pl.when(b > 0)
        def _():
            x_copy(0, f, 0).start()

    moves[4].wait()
    for f in range(3):
        for p in range(cx):
            zs[0, f, p] = vel[2, p] * field[f, p]
        for side in range(2):
            z_copy(0, f, side).start()

    for move in moves[5:]:
        move.wait()
    cells = cell_ref[...]
    cell_row = cells // cz
    cell_lane = cells - cell_row * cz
    row_ids = lax.broadcasted_iota(jnp.int32, (cx * cy, capacity), 0)
    onehot[...] = jnp.where(row_ids == cell_row, 1.0, 0.0).astype(bf16)
    lane_ids = lax.broadcasted_iota(jnp.int32, (cz, capacity), 0)
    lane_hit = lane_ids == cell_lane
    picked = []
    for f in range(3):
        high, low = split(field[f].reshape(cx * cy, cz))
        found = dot(high, onehot[...], ((0,), (0,))) + dot(low, onehot[...], ((0,), (0,)))
        picked.append(jnp.sum(jnp.where(lane_hit, found, 0.0), axis=0, keepdims=True))
    rho, eps, lam = picked
    weak_row = 0.62 + 0.04 * rho + 0.05 * (lam / rho)
    capture_row = 0.3 * jax.nn.sigmoid(eps / rho)
    for k in range(capacity // 128):
        part = pl.ds(k * 128, 128)
        cols = slice(k * 128, k * 128 + 128)
        rate_weak[part, :] = jnp.broadcast_to(weak_row[:, cols], (128, 128)).T
        rate_capture[part, :] = jnp.broadcast_to(capture_row[:, cols], (128, 128)).T

    for k in range(2):
        high, low = split(rates[k])
        cols = pl.ds(k * species, species)
        weights[0:species, cols] = high
        weights[species : 2 * species, cols] = high
        weights[2 * species : 3 * species, cols] = low

    count = count_ref[...]
    for k in range(capacity // BLOCK):
        part = pl.ds(k * BLOCK, BLOCK)
        row = lax.broadcasted_iota(jnp.int32, (BLOCK, species), 0) + k * BLOCK
        first = jnp.where(row < count, start_rows[part, :], 0.0)
        start_rows[part, :] = first
        abundance_out[part, :] = first

    def product(values):
        high, low = split(values)
        return dot(jnp.concatenate([high, low, high], axis=1), weights[...])

    def newton_start(turn):
        for k in range(capacity // BLOCK):
            part = pl.ds(k * BLOCK, BLOCK)
            now = abundance_out[part, :]
            made = product(now)
            capture = made[:, species:]
            scaled = rate_capture[part, :]
            alpha = scaled * now[:, 0:1]
            alpha_capture[part, :] = alpha
            scaled_capture[part, :] = scaled * capture
            aim = rate_weak[part, :] * made[:, :species] + alpha * capture
            if turn:
                aim = aim - (now - start_rows[part, :])
            target[part, :] = aim
            update[part, :] = aim

    def sweeps(number):
        def sweep(_, carry):
            for k in range(capacity // BLOCK):
                part = pl.ds(k * BLOCK, BLOCK)
                now = update[part, :]
                made = product(now)
                update[part, :] = target[part, :] + (
                    rate_weak[part, :] * made[:, :species]
                    + alpha_capture[part, :] * made[:, species:]
                    + scaled_capture[part, :] * now[:, 0:1]
                )
            return carry

        lax.fori_loop(0, number, sweep, 0)

    def newton_end():
        for k in range(capacity // BLOCK):
            part = pl.ds(k * BLOCK, BLOCK)
            abundance_out[part, :] = abundance_out[part, :] + update[part, :]

    half = 0.5 * courant / 12.0
    full = courant / 12.0

    def inside(stage, f, quantity, flux):
        results = []
        for p in range(cx):
            total = y_part(vel[1, p] * quantity[p]) + z_part(zs[stage, f, p], z_in[stage, f, p])
            for step, factor in ((1, 8.0), (-1, -8.0), (2, -1.0), (-2, 1.0)):
                if 0 <= p + step < cx:
                    total = total + factor * flux[p + step]
            results.append(total)
        return results

    def from_low(stage, f):
        near, far = low_in[stage, f, 1], low_in[stage, f, 0]
        return far - 8.0 * near, near

    def from_high(stage, f):
        near, far = high_in[stage, f, 0], high_in[stage, f, 1]
        return -near, 8.0 * near - far

    def half_inside(f):
        for side in range(2):
            z_copy(0, f, side).wait_recv()
        slopes = inside(0, f, [field[f, p] for p in range(cx)], [xs[0, f, p] for p in range(cx)])
        for p in range(cx):
            mid[f, p] = field[f, p] - half * slopes[p]

    def send_flux(f, side):
        for p in (0, 1) if side == 0 else (cx - 2, cx - 1):
            xs[1, f, p] = vel[0, p] * mid[f, p]
        x_copy(1, f, side).start()

    def finish_half(f, side, send=True):
        x_copy(0, f, 1 - side).wait_recv()
        extra = from_low(0, f) if side == 0 else from_high(0, f)
        for p, part in zip((0, 1) if side == 0 else (cx - 2, cx - 1), extra):
            value = mid[f, p] - half * part
            mid[f, p] = value
            if send:
                xs[1, f, p] = vel[0, p] * value
            zs[1, f, p] = vel[2, p] * value
        if send:
            x_copy(1, f, side).start()
        z_copy(1, f, side).start()

    def finish_half_sides(f):
        @pl.when(b < last)
        def _():
            finish_half(f, 1)

        @pl.when(b > 0)
        def _():
            finish_half(f, 0)

    newton_start(0)
    sweeps(EARLY)
    for f in range(3):
        half_inside(f)

    @pl.when(b == last)
    def _():
        for f in range(3):
            send_flux(f, 1)
        v_copy().start()

    finish_half_sides(0)
    sweeps(SWEEPS - EARLY)
    newton_end()
    newton_start(1)

    @pl.when(b == 0)
    def _():
        pl.semaphore_wait(barrier, 1)
        for f in range(3):
            x_copy(0, f, 0).start()

    finish_half_sides(1)
    sweeps(SWEEPS // 2)
    finish_half_sides(2)
    sweeps(SWEEPS - SWEEPS // 2)
    newton_end()

    change_high, change_low = split(abundance_out[...] - start_rows[...])
    pair = jnp.concatenate([table[...], jnp.zeros((6, species), f32)], axis=0)
    table_high, table_low = split(pair)
    gains = (
        dot(table_high, change_high, ((1,), (1,)))
        + dot(table_high, change_low, ((1,), (1,)))
        + dot(table_low, change_high, ((1,), (1,)))
    ) * mass_ref[...]
    for k in range(2):
        placed = jnp.where(lane_ids == cell_lane, gains[k : k + 1, :], 0.0)
        high, low = split(placed)
        deposit[k] = (
            dot(onehot[...], high, ((1,), (1,))) + dot(onehot[...], low, ((1,), (1,)))
        ).reshape(cx, cy, cz)

    @pl.when(b == 0)
    def _():
        for f in range(3):
            finish_half(f, 0)

    @pl.when(b == last)
    def _():
        for f in range(3):
            finish_half(f, 1, send=False)

    for f in range(3):
        for side in range(2):
            z_copy(1, f, side).wait_recv()
        slopes = inside(
            1, f, [mid[f, p] for p in range(cx)], [vel[0, p] * mid[f, p] for p in range(cx)]
        )
        for p in range(cx):
            value = field[f, p] - full * slopes[p]
            if f:
                value = value + deposit[f - 1, p]
            outs[f][p] = value

    @pl.when(b == 0)
    def _():
        v_copy().wait_recv()

    for f in range(3):
        for side in range(2):
            x_copy(1, f, side).wait_recv()

        @pl.when(b == 0)
        def _():
            share = (-xs[0, f, 0], 8.0 * xs[0, f, 0] - xs[0, f, 1])
            for p in range(2):
                low_in[1, f, p] = low_in[1, f, p] - half * v_in[p] * share[p]

        for p, part in enumerate(from_low(1, f) + from_high(1, f)):
            outs[f][p] = outs[f][p] - full * part

    for stage in range(2):
        for f in range(3):
            for side in range(2):
                x_copy(stage, f, side).wait_send()
                z_copy(stage, f, side).wait_send()

    @pl.when(b == last)
    def _():
        v_copy().wait_send()


def settle(a_ref, b_ref, c_ref, d_ref, a_out, b_out, c_out, d_out, sem):
    pairs = ((d_ref, d_out), (a_ref, a_out), (b_ref, b_out), (c_ref, c_out))
    moves = [pltpu.make_async_copy(src, dst, sem.at[k]) for k, (src, dst) in enumerate(pairs)]
    for move in moves:
        move.start()
    for move in moves:
        move.wait()


def on_device(
    axis_sizes,
    density,
    energy_field,
    lepton_field,
    velocity,
    abundance,
    tracer_mass,
    tracer_cell,
    tracer_count,
    weak_rates,
    capture_rates,
    binding,
    charge_ratio,
):
    cx, cy, cz = density.shape
    capacity, species = abundance.shape[2:]
    vmem = pl.BlockSpec(memory_space=pltpu.VMEM)
    field = jax.ShapeDtypeStruct(density.shape, f32)
    rows = pltpu.VMEM((capacity, species), f32)
    advanced = pl.pallas_call(
        functools.partial(kernel, axis_sizes),
        out_shape=(pltpu.VMEM(density.shape, f32),) * 3 + (rows,),
        in_specs=[pl.BlockSpec(memory_space=pl.ANY)] * 12,
        out_specs=(vmem,) * 4,
        scratch_shapes=[
            pltpu.VMEM((1, 1), jnp.int32),
            pltpu.VMEM((3, cx, cy, cz), f32),
            pltpu.VMEM((3, cx, cy, cz), f32),
            pltpu.VMEM((1, capacity), f32),
            pltpu.VMEM((1, capacity), jnp.int32),
            pltpu.VMEM((2, species, species), f32),
            pltpu.VMEM((2, species), f32),
            pltpu.VMEM((2, 3, cx, cy, cz), f32),
            pltpu.VMEM((2, 3, cx, cy, cz), f32),
            pltpu.VMEM((2, 3, 2, cy, cz), f32),
            pltpu.VMEM((2, 3, 2, cy, cz), f32),
            pltpu.VMEM((2, 3, cx, cy, cz), f32),
            pltpu.VMEM((2, cy, cz), f32),
            pltpu.VMEM((3, cx, cy, cz), f32),
            pltpu.VMEM((3 * species, 2 * species), bf16),
            pltpu.VMEM((cx * cy, capacity), bf16),
            rows,
            rows,
            rows,
            rows,
            rows,
            rows,
            rows,
            pltpu.VMEM((2, cx, cy, cz), f32),
            pltpu.SemaphoreType.DMA((14,)),
            pltpu.SemaphoreType.DMA((2, 3, 2)),
            pltpu.SemaphoreType.DMA((2, 3, 2)),
            pltpu.SemaphoreType.DMA((2, 3, 2)),
            pltpu.SemaphoreType.DMA((2, 3, 2)),
            pltpu.SemaphoreType.DMA((2,)),
        ],
        compiler_params=pltpu.CompilerParams(collective_id=0, has_side_effects=True),
    )(
        tracer_count,
        density,
        energy_field,
        lepton_field,
        velocity,
        abundance.reshape(capacity, species),
        tracer_mass.reshape(1, capacity),
        tracer_cell.reshape(1, capacity),
        weak_rates,
        capture_rates,
        binding.reshape(1, species),
        charge_ratio.reshape(1, species),
    )
    whole = pl.BlockSpec(memory_space=pl.ANY)
    results = pl.pallas_call(
        settle,
        out_shape=(field, field, field, jax.ShapeDtypeStruct((capacity, species), f32)),
        in_specs=[whole] * 4,
        out_specs=(whole,) * 4,
        scratch_shapes=[pltpu.SemaphoreType.DMA((4,))],
    )(*[pltpu.with_memory_space_constraint(a, pltpu.VMEM) for a in advanced])
    return results[0], results[1], results[2], results[3][None, None]


def solution(mesh):
    sizes = (mesh.shape["grp"], mesh.shape["brick"])
    assert sizes[0] == 2
    return jax.shard_map(
        functools.partial(on_device, sizes),
        mesh=mesh,
        in_specs=(
            P("brick", None, "grp"),
            P("brick", None, "grp"),
            P("brick", None, "grp"),
            P(None, "brick", None, "grp"),
            P("grp", "brick", None, None),
            P("grp", "brick", None),
            P("grp", "brick", None),
            P("grp", "brick"),
            P(),
            P(),
            P(),
            P(),
        ),
        out_specs=(
            P("brick", None, "grp"),
            P("brick", None, "grp"),
            P("brick", None, "grp"),
            P("grp", "brick", None, None),
        ),
        check_vma=False,
    )
```

```python
import functools

import jax
import jax.numpy as jnp
from jax import lax
from jax.experimental import pallas as pl
from jax.experimental.pallas import tpu as pltpu
from jax.sharding import PartitionSpec as P

NEWTON = 2
SWEEPS = 8
courant = 0.8
f32 = jnp.float32
bf16 = jnp.bfloat16
BLOCK = 256
ROW = 4
MESH = pl.DeviceIdType.MESH


def split(values):
    high = values.astype(bf16)
    low = (values - high.astype(f32)).astype(bf16)
    return high, low


def dot(a, b, dims=((1,), (0,))):
    return lax.dot_general(a, b, (dims, ((), ())), preferred_element_type=f32)


def five_point(lower2, lower1, upper1, upper2):
    return 8.0 * (upper1 - lower1) - (upper2 - lower2)


def y_part(g):
    n = g.shape[0]
    return five_point(
        pltpu.roll(g, 2, 0), pltpu.roll(g, 1, 0), pltpu.roll(g, n - 1, 0), pltpu.roll(g, n - 2, 0)
    )


def z_part(h, other):
    n = h.shape[1]
    lane = lax.broadcasted_iota(jnp.int32, h.shape, 1)
    return five_point(
        pltpu.roll(jnp.where(lane >= n - 2, other, h), 2, 1),
        pltpu.roll(jnp.where(lane >= n - 1, other, h), 1, 1),
        pltpu.roll(jnp.where(lane < 1, other, h), n - 1, 1),
        pltpu.roll(jnp.where(lane < 2, other, h), n - 2, 1),
    )


def kernel(
    axis_sizes,
    count_hbm,
    rho_hbm,
    eps_hbm,
    lam_hbm,
    vel_hbm,
    rows_hbm,
    mass_hbm,
    cell_hbm,
    weak_hbm,
    capture_hbm,
    binding_hbm,
    charge_hbm,
    density_out,
    energy_out,
    lepton_out,
    abundance_out,
    count_ref,
    field,
    vel,
    mass_ref,
    cell_ref,
    rates,
    table,
    xs,
    zs,
    low_in,
    high_in,
    z_in,
    v_in,
    mid,
    weights,
    onehot,
    rate_weak,
    rate_capture,
    start_rows,
    alpha_capture,
    scaled_capture,
    target,
    update,
    deposit,
    load_sem,
    send_sem,
    recv_sem,
    z_send_sem,
    z_recv_sem,
    v_sem,
):
    n_grp, n_brick = axis_sizes
    g = lax.axis_index("grp")
    b = lax.axis_index("brick")
    last = n_brick - 1
    spot = lax.rem(b, ROW)
    right = (g, lax.rem(b + 1, n_brick))
    left = (g, lax.rem(b + n_brick - 1, n_brick))
    partner = (lax.rem(g + 1, n_grp), b)
    outs = (density_out, energy_out, lepton_out)
    cx, cy, cz = density_out.shape
    capacity, species = abundance_out.shape
    assert cx == 4
    low_pair = pl.ds(0, 2)
    high_pair = pl.ds(cx - 2, 2)
    pairs = (low_pair, high_pair)

    barrier = pltpu.get_barrier_semaphore()

    def greet(device):
        pl.semaphore_signal(barrier, inc=1, device_id=device, device_id_type=MESH)

    greet(partner)

    @pl.when(b > 0)
    def _():
        greet(left)

    @pl.when(b < last)
    def _():
        greet(right)

    moves = [
        pltpu.make_async_copy(src, dst, load_sem.at[k])
        for k, (src, dst) in enumerate(
            (
                (vel_hbm.at[0], vel.at[0]),
                (rho_hbm, field.at[0]),
                (eps_hbm, field.at[1]),
                (lam_hbm, field.at[2]),
                (vel_hbm.at[2], vel.at[2]),
                (cell_hbm, cell_ref),
                (vel_hbm.at[1], vel.at[1]),
                (weak_hbm, rates.at[0]),
                (capture_hbm, rates.at[1]),
                (count_hbm, count_ref),
                (rows_hbm, start_rows),
                (mass_hbm, mass_ref),
                (binding_hbm, table.at[pl.ds(0, 1)]),
                (charge_hbm, table.at[pl.ds(1, 1)]),
            )
        )
    ]
    for move in moves:
        move.start()

    def x_copy(stage, f, side):
        src, dst, device = (
            (xs.at[stage, f, low_pair], high_in.at[stage, f], left),
            (xs.at[stage, f, high_pair], low_in.at[stage, f], right),
        )[side]
        return pltpu.make_async_remote_copy(
            src_ref=src,
            dst_ref=dst,
            send_sem=send_sem.at[stage, f, side],
            recv_sem=recv_sem.at[stage, f, side],
            device_id=device,
            device_id_type=MESH,
        )

    def z_copy(stage, f, side):
        return pltpu.make_async_remote_copy(
            src_ref=zs.at[stage, f, pairs[side]],
            dst_ref=z_in.at[stage, f, pairs[side]],
            send_sem=z_send_sem.at[stage, f, side],
            recv_sem=z_recv_sem.at[stage, f, side],
            device_id=partner,
            device_id_type=MESH,
        )

    def v_copy():
        return pltpu.make_async_remote_copy(
            src_ref=vel.at[0, high_pair],
            dst_ref=v_in,
            send_sem=v_sem.at[0],
            recv_sem=v_sem.at[1],
            device_id=right,
            device_id_type=MESH,
        )

    moves[0].wait()
    for f in range(3):
        moves[1 + f].wait()
        for p in range(cx):
            xs[0, f, p] = vel[0, p] * field[f, p]

    @pl.when(b == 0)
    def _():
        pl.semaphore_wait(barrier, 2)
        greet(left)

    @pl.when(b > 0)
    def _():
        pl.semaphore_wait(barrier, 3)

    @pl.when(b == last)
    def _():
        greet(right)

    def at(*spots):
        found = spot == spots[0]
        for other in spots[1:]:
            found = jnp.logical_or(found, spot == other)
        return found

    far_left = jnp.logical_and(spot == 0, b > 0)
    far_right = jnp.logical_and(spot == ROW - 1, b < last)

    def send_near(f):
        @pl.when(at(0, 1))
        def _():
            x_copy(0, f, 1).start()

        @pl.when(at(1, 2))
        def _():
            x_copy(0, f, 0).start()

        @pl.when(at(3))
        def _():
            x_copy(0, f, 0).start()

        @pl.when(at(2))
        def _():
            x_copy(0, f, 1).start()

    def send_far(f):
        @pl.when(far_left)
        def _():
            x_copy(0, f, 0).start()

        @pl.when(far_right)
        def _():
            x_copy(0, f, 1).start()

    def send_seam(f):
        @pl.when(b == last)
        def _():
            x_copy(0, f, 1).start()

    send_near(0)

    send_far(0)
    send_seam(0)

    moves[4].wait()
    for f in range(3):
        for p in range(cx):
            zs[0, f, p] = vel[2, p] * field[f, p]
        for side in range(2):
            z_copy(0, f, side).start()

    for move in moves[5:]:
        move.wait()
    cells = cell_ref[...]
    cell_row = cells // cz
    cell_lane = cells - cell_row * cz
    row_ids = lax.broadcasted_iota(jnp.int32, (cx * cy, capacity), 0)
    onehot[...] = jnp.where(row_ids == cell_row, 1.0, 0.0).astype(bf16)
    lane_ids = lax.broadcasted_iota(jnp.int32, (cz, capacity), 0)
    lane_hit = lane_ids == cell_lane
    picked = []
    for f in range(3):
        high, low = split(field[f].reshape(cx * cy, cz))
        found = dot(high, onehot[...], ((0,), (0,))) + dot(low, onehot[...], ((0,), (0,)))
        picked.append(jnp.sum(jnp.where(lane_hit, found, 0.0), axis=0, keepdims=True))
    rho, eps, lam = picked
    weak_row = 0.62 + 0.04 * rho + 0.05 * (lam / rho)
    capture_row = 0.3 * jax.nn.sigmoid(eps / rho)
    for k in range(capacity // 128):
        part = pl.ds(k * 128, 128)
        cols = slice(k * 128, k * 128 + 128)
        rate_weak[part, :] = jnp.broadcast_to(weak_row[:, cols], (128, 128)).T
        rate_capture[part, :] = jnp.broadcast_to(capture_row[:, cols], (128, 128)).T

    for k in range(2):
        high, low = split(rates[k])
        cols = pl.ds(k * species, species)
        weights[0:species, cols] = high
        weights[species : 2 * species, cols] = high
        weights[2 * species : 3 * species, cols] = low

    count = count_ref[...]
    for k in range(capacity // BLOCK):
        part = pl.ds(k * BLOCK, BLOCK)
        row = lax.broadcasted_iota(jnp.int32, (BLOCK, species), 0) + k * BLOCK
        first = jnp.where(row < count, start_rows[part, :], 0.0)
        start_rows[part, :] = first
        abundance_out[part, :] = first

    def product(values):
        high, low = split(values)
        return dot(jnp.concatenate([high, low, high], axis=1), weights[...])

    def newton_start(turn):
        for k in range(capacity // BLOCK):
            part = pl.ds(k * BLOCK, BLOCK)
            now = abundance_out[part, :]
            made = product(now)
            capture = made[:, species:]
            scaled = rate_capture[part, :]
            alpha = scaled * now[:, 0:1]
            alpha_capture[part, :] = alpha
            scaled_capture[part, :] = scaled * capture
            aim = rate_weak[part, :] * made[:, :species] + alpha * capture
            if turn:
                aim = aim - (now - start_rows[part, :])
            target[part, :] = aim
            update[part, :] = aim

    def sweeps(number):
        def sweep(_, carry):
            for k in range(capacity // BLOCK):
                part = pl.ds(k * BLOCK, BLOCK)
                now = update[part, :]
                made = product(now)
                update[part, :] = target[part, :] + (
                    rate_weak[part, :] * made[:, :species]
                    + alpha_capture[part, :] * made[:, species:]
                    + scaled_capture[part, :] * now[:, 0:1]
                )
            return carry

        lax.fori_loop(0, number, sweep, 0)

    def newton_end():
        for k in range(capacity // BLOCK):
            part = pl.ds(k * BLOCK, BLOCK)
            abundance_out[part, :] = abundance_out[part, :] + update[part, :]

    half = 0.5 * courant / 12.0
    full = courant / 12.0

    def inside(stage, f, quantity, flux):
        results = []
        for p in range(cx):
            total = y_part(vel[1, p] * quantity[p]) + z_part(zs[stage, f, p], z_in[stage, f, p])
            for step, factor in ((1, 8.0), (-1, -8.0), (2, -1.0), (-2, 1.0)):
                if 0 <= p + step < cx:
                    total = total + factor * flux[p + step]
            results.append(total)
        return results

    def from_low(stage, f):
        near, far = low_in[stage, f, 1], low_in[stage, f, 0]
        return far - 8.0 * near, near

    def from_high(stage, f):
        near, far = high_in[stage, f, 0], high_in[stage, f, 1]
        return -near, 8.0 * near - far

    def half_inside(f):
        for side in range(2):
            z_copy(0, f, side).wait_recv()
        slopes = inside(0, f, [field[f, p] for p in range(cx)], [xs[0, f, p] for p in range(cx)])
        for p in range(cx):
            mid[f, p] = field[f, p] - half * slopes[p]

    def send_flux(f, side):
        for p in (0, 1) if side == 0 else (cx - 2, cx - 1):
            xs[1, f, p] = vel[0, p] * mid[f, p]
        x_copy(1, f, side).start()

    def finish_half(f, side, send=True):
        x_copy(0, f, 1 - side).wait_recv()
        extra = from_low(0, f) if side == 0 else from_high(0, f)
        for p, part in zip((0, 1) if side == 0 else (cx - 2, cx - 1), extra):
            value = mid[f, p] - half * part
            mid[f, p] = value
            if send:
                xs[1, f, p] = vel[0, p] * value
            zs[1, f, p] = vel[2, p] * value
        if send:
            x_copy(1, f, side).start()
        z_copy(1, f, side).start()

    held_up = b == ROW - 2

    def finish_near(f):
        @pl.when(at(1, 2, 3) if f == 2 else at(2, 3))
        def _():
            finish_half(f, 0)

        @pl.when(jnp.logical_and(at(0, 1, 2), jnp.logical_not(held_up)) if f else at(0, 1, 2))
        def _():
            finish_half(f, 1)

        if f < 2:

            @pl.when(at(1))
            def _():
                finish_half(f, 0)

    def finish_held_up(f):
        @pl.when(held_up)
        def _():
            finish_half(f, 1)

    def finish_far(f):
        @pl.when(far_left)
        def _():
            finish_half(f, 0)

        @pl.when(far_right)
        def _():
            finish_half(f, 1)

    def seam_flux(f):
        @pl.when(b == last)
        def _():
            send_flux(f, 1)
            if f == 0:
                v_copy().start()

    def seam_back(f):
        @pl.when(b == 0)
        def _():
            if f == 0:
                pl.semaphore_wait(barrier, 1)
            x_copy(0, f, 0).start()

    def seam_half(f):
        @pl.when(b == 0)
        def _():
            finish_half(f, 0)

    send_near(1)
    send_seam(1)
    newton_start(0)
    sweeps(2)
    send_far(1)
    send_seam(2)
    for f in range(3):
        half_inside(f)
    send_near(2)
    seam_back(0)
    finish_near(0)
    sweeps(3)
    send_far(2)
    seam_flux(0)
    seam_back(1)
    sweeps(SWEEPS - 5)
    newton_end()
    newton_start(1)
    finish_near(1)
    finish_far(0)
    seam_flux(1)
    seam_flux(2)
    seam_back(2)
    sweeps(SWEEPS // 2)
    finish_near(2)
    seam_half(0)
    sweeps(2)
    finish_far(1)
    finish_held_up(1)
    seam_half(1)
    sweeps(SWEEPS - SWEEPS // 2 - 2)
    newton_end()
    seam_half(2)

    change_high, change_low = split(abundance_out[...] - start_rows[...])
    pair = jnp.concatenate([table[...], jnp.zeros((6, species), f32)], axis=0)
    table_high, table_low = split(pair)
    gains = (
        dot(table_high, change_high, ((1,), (1,)))
        + dot(table_high, change_low, ((1,), (1,)))
        + dot(table_low, change_high, ((1,), (1,)))
    ) * mass_ref[...]
    for k in range(2):
        placed = jnp.where(lane_ids == cell_lane, gains[k : k + 1, :], 0.0)
        high, low = split(placed)
        deposit[k] = (
            dot(onehot[...], high, ((1,), (1,))) + dot(onehot[...], low, ((1,), (1,)))
        ).reshape(cx, cy, cz)

    finish_far(2)
    finish_held_up(2)

    @pl.when(b == last)
    def _():
        for f in range(3):
            finish_half(f, 1, send=False)

    for f in range(3):
        for side in range(2):
            z_copy(1, f, side).wait_recv()
        slopes = inside(
            1, f, [mid[f, p] for p in range(cx)], [vel[0, p] * mid[f, p] for p in range(cx)]
        )
        for p in range(cx):
            value = field[f, p] - full * slopes[p]
            if f:
                value = value + deposit[f - 1, p]
            outs[f][p] = value

    @pl.when(b == 0)
    def _():
        v_copy().wait_recv()

    for f in range(3):
        for side in range(2):
            x_copy(1, f, side).wait_recv()

        @pl.when(b == 0)
        def _():
            share = (-xs[0, f, 0], 8.0 * xs[0, f, 0] - xs[0, f, 1])
            for p in range(2):
                low_in[1, f, p] = low_in[1, f, p] - half * v_in[p] * share[p]

        for p, part in enumerate(from_low(1, f) + from_high(1, f)):
            outs[f][p] = outs[f][p] - full * part

    for stage in range(2):
        for f in range(3):
            for side in range(2):
                x_copy(stage, f, side).wait_send()
                z_copy(stage, f, side).wait_send()

    @pl.when(b == last)
    def _():
        v_copy().wait_send()


def settle(a_ref, b_ref, c_ref, d_ref, a_out, b_out, c_out, d_out, sem):
    pairs = ((d_ref, d_out), (a_ref, a_out), (b_ref, b_out), (c_ref, c_out))
    moves = [pltpu.make_async_copy(src, dst, sem.at[k]) for k, (src, dst) in enumerate(pairs)]
    for move in moves:
        move.start()
    for move in moves:
        move.wait()


def on_device(
    axis_sizes,
    density,
    energy_field,
    lepton_field,
    velocity,
    abundance,
    tracer_mass,
    tracer_cell,
    tracer_count,
    weak_rates,
    capture_rates,
    binding,
    charge_ratio,
):
    cx, cy, cz = density.shape
    capacity, species = abundance.shape[2:]
    vmem = pl.BlockSpec(memory_space=pltpu.VMEM)
    field = jax.ShapeDtypeStruct(density.shape, f32)
    rows = pltpu.VMEM((capacity, species), f32)
    advanced = pl.pallas_call(
        functools.partial(kernel, axis_sizes),
        out_shape=(pltpu.VMEM(density.shape, f32),) * 3 + (rows,),
        in_specs=[pl.BlockSpec(memory_space=pl.ANY)] * 12,
        out_specs=(vmem,) * 4,
        scratch_shapes=[
            pltpu.VMEM((1, 1), jnp.int32),
            pltpu.VMEM((3, cx, cy, cz), f32),
            pltpu.VMEM((3, cx, cy, cz), f32),
            pltpu.VMEM((1, capacity), f32),
            pltpu.VMEM((1, capacity), jnp.int32),
            pltpu.VMEM((2, species, species), f32),
            pltpu.VMEM((2, species), f32),
            pltpu.VMEM((2, 3, cx, cy, cz), f32),
            pltpu.VMEM((2, 3, cx, cy, cz), f32),
            pltpu.VMEM((2, 3, 2, cy, cz), f32),
            pltpu.VMEM((2, 3, 2, cy, cz), f32),
            pltpu.VMEM((2, 3, cx, cy, cz), f32),
            pltpu.VMEM((2, cy, cz), f32),
            pltpu.VMEM((3, cx, cy, cz), f32),
            pltpu.VMEM((3 * species, 2 * species), bf16),
            pltpu.VMEM((cx * cy, capacity), bf16),
            rows,
            rows,
            rows,
            rows,
            rows,
            rows,
            rows,
            pltpu.VMEM((2, cx, cy, cz), f32),
            pltpu.SemaphoreType.DMA((14,)),
            pltpu.SemaphoreType.DMA((2, 3, 2)),
            pltpu.SemaphoreType.DMA((2, 3, 2)),
            pltpu.SemaphoreType.DMA((2, 3, 2)),
            pltpu.SemaphoreType.DMA((2, 3, 2)),
            pltpu.SemaphoreType.DMA((2,)),
        ],
        compiler_params=pltpu.CompilerParams(collective_id=0, has_side_effects=True),
    )(
        tracer_count,
        density,
        energy_field,
        lepton_field,
        velocity,
        abundance.reshape(capacity, species),
        tracer_mass.reshape(1, capacity),
        tracer_cell.reshape(1, capacity),
        weak_rates,
        capture_rates,
        binding.reshape(1, species),
        charge_ratio.reshape(1, species),
    )
    whole = pl.BlockSpec(memory_space=pl.ANY)
    results = pl.pallas_call(
        settle,
        out_shape=(field, field, field, jax.ShapeDtypeStruct((capacity, species), f32)),
        in_specs=[whole] * 4,
        out_specs=(whole,) * 4,
        scratch_shapes=[pltpu.SemaphoreType.DMA((4,))],
    )(*[pltpu.with_memory_space_constraint(a, pltpu.VMEM) for a in advanced])
    return results[0], results[1], results[2], results[3][None, None]


def solution(mesh):
    sizes = (mesh.shape["grp"], mesh.shape["brick"])
    assert sizes[0] == 2
    return jax.shard_map(
        functools.partial(on_device, sizes),
        mesh=mesh,
        in_specs=(
            P("brick", None, "grp"),
            P("brick", None, "grp"),
            P("brick", None, "grp"),
            P(None, "brick", None, "grp"),
            P("grp", "brick", None, None),
            P("grp", "brick", None),
            P("grp", "brick", None),
            P("grp", "brick"),
            P(),
            P(),
            P(),
            P(),
        ),
        out_specs=(
            P("brick", None, "grp"),
            P("brick", None, "grp"),
            P("brick", None, "grp"),
            P("grp", "brick", None, None),
        ),
        check_vma=False,
    )
```
